32 devices in a mesh: span: 4 (over z), flow: 8 (over y, x, core).
Axes of the slice: x: 2, y: 2, z: 4, core: 2. Of those that a mesh axis runs over, the one named last changes fastest.
Arguments:
- rhs_fluid: float32 [6, 8, 64, 128], P(None, 'span', 'flow'), may hold values from -6 to 6
- rhs_solid: float32 [32, 128], P('span'), may hold values from -6 to 6
- blocks: float32 [6, 6, 8, 64, 128], P(None, None, 'span', 'flow')
- weights: float32 [6, 8, 64, 128], P(None, 'span', 'flow'), may hold values from 0.5 to 1.1
- kdiag: float32 [32, 128], P('span'), may hold values from 1 to 4
- wall_fluid: int32 [4, 8], P('span', 'flow'), may hold values from 0 to 15
- wall_solid: int32 [4, 8], P('span', 'flow'), may hold values from 0 to 7, each once within a row
- wall_coef: float32 [4, 8, 128], P('span', 'flow'), may hold values from 0.3 to 1.5
Outputs:
- x_fluid: float32 [6, 8, 64, 128], P(None, 'span', 'flow')
- x_solid: float32 [32, 128], P('span')
The draws below stay inside these ranges and needn't reach their ends.
Inputs may be any that keep to these rules, and one draw needn't show every extreme that they name: `wall_fluid`: a local row a * 8 + b of the fluid tile of span index i and flow index q; rows may repeat. `wall_solid`: each row is a permutation of the 8 metal rows of band i.
All inputs are finite; a program needn't handle non-finite values.
Results may differ from the reference program's by a relative error of at most 0.0003.
Values sent between devices are 32-bit elements; how exact they have to be, the bound alone decides.
No kernel may reach another device: no remote copies, remote signals or barrier semaphores. Data moves between devices by JAX's collectives and lax.ppermute only.
A program may use at most 64 MiB of HBM per device.

```python
import math
import jax
import jax.numpy as jnp
from jax import lax

FIELDS = 6
CA = 2
CB = 8
NC = 128
K = 1
KRYLOV = 6
NA = 8
NB = 64
SROWS = 8
NSOL = 32
N_SPAN = 4


def draw_blocks(key, part):
    key_diag = jax.random.fold_in(key, 11)
    key_off = jax.random.fold_in(key, 12)
    diag_part = jax.random.uniform(key_diag, (6, NA, NB, NC), jnp.float32, 8.0, 10.0)
    off_part = 0.3 * jax.random.normal(key_off, (6, 6, NA, NB, NC), jnp.float32)
    off_part = jnp.clip(off_part, -0.45, 0.45)
    unit = jnp.eye(6, dtype=jnp.float32)[:, :, None, None, None]
    return off_part * (1.0 - unit) + unit * diag_part[:, None]


def with_ends(result, rng, least, largest):
    spot = [jax.random.randint(jax.random.fold_in(rng, axis), (), 0, length) for axis, length in enumerate(result.shape)]
    main_axis = result.shape.index(max(result.shape))
    neighbour = spot[:main_axis] + [(spot[main_axis] + 1) % result.shape[main_axis]] + spot[main_axis + 1:]
    return result.at[tuple(spot)].set(least).at[tuple(neighbour)].set(largest)


def block_levels(own_key, extent, split, smallest, high):
    factor_of = 1.0
    for position, parts in split:
        draws = jax.random.uniform(jax.random.fold_in(jax.random.fold_in(own_key, 6), position), (parts,), jnp.float32, smallest / len(split), high / len(split))
        factor_of = factor_of * jnp.repeat(jnp.exp(draws), extent[position] // parts).reshape((-1,) + (1,) * (len(extent) - 1 - position))
    return factor_of


def bell_draw(stream_key, shape, spread, reach, split=(), kind=jnp.bfloat16):
    gain = block_levels(stream_key, shape, split, -0.22, 0.18) if split else 1.0
    entries = jax.random.normal(stream_key, shape, jnp.float32) * spread * gain
    return jnp.minimum(jnp.maximum(entries, -reach), reach).astype(kind)


def setup_inputs(seed: int = 0) -> dict:
    seeds = jax.random.split(jax.random.key(seed), 9)
    rhs_fluid = bell_draw(seeds[0], (FIELDS, NA, NB, NC), 1.0, 6.0, ((1, 4), (2, 8)), jnp.float32)
    rhs_solid = bell_draw(seeds[1], (NSOL, NC), 1.0, 6.0, ((0, 4),), jnp.float32)
    blocks = draw_blocks(jax.random.fold_in(seeds[8], 71), 0)
    weights = jnp.clip(0.5 + 0.6 * jax.random.uniform(seeds[3], (6, NA, NB, NC), jnp.float32) ** block_levels(seeds[3], (6, NA, NB, NC), ((1, 4), (2, 8)), -0.2, 0.2), 0.5, 1.1)
    kdiag = jnp.clip(jnp.exp(math.log(4.0) - 1.3862944 * jax.random.uniform(seeds[4], (NSOL, NC), jnp.float32) ** block_levels(seeds[4], (NSOL, NC), ((0, 4),), -0.2, 0.2)), 1.0, 4.0)
    wall_fluid = with_ends(jax.random.randint(seeds[5], (N_SPAN, SROWS), 0, CA * CB), jax.random.fold_in(seeds[5], 1), 0, (CA * CB) - 1).astype(jnp.int32)
    wall_solid = jax.vmap(lambda own: jax.random.permutation(own, SROWS))(jax.random.split(seeds[6], N_SPAN)).reshape((N_SPAN, SROWS)).astype(jnp.int32)
    wall_coef = jnp.clip(jnp.exp(math.log(1.5) - 1.60943787 * jax.random.uniform(seeds[7], (N_SPAN, SROWS, NC), jnp.float32) ** block_levels(seeds[7], (N_SPAN, SROWS, NC), ((0, 4), (1, 8)), -0.2, 0.2)), 0.3, 1.5)
    return {"rhs_fluid": rhs_fluid, "rhs_solid": rhs_solid, "blocks": blocks, "weights": weights, "kdiag": kdiag, "wall_fluid": wall_fluid, "wall_solid": wall_solid, "wall_coef": wall_coef}


def patch_index(wall_fluid, wall_solid):
    band = jnp.arange(N_SPAN, dtype=jnp.int32)[:, None]
    slot = jnp.arange(SROWS, dtype=jnp.int32)[None, :]
    fluid_a = (band * CA + wall_fluid // CB).reshape(-1)
    fluid_b = (slot // K * CB + wall_fluid % CB).reshape(-1)
    metal = (band * SROWS + wall_solid).reshape(-1)
    return (fluid_a, fluid_b, metal)

def apply_all(field, metal_u, blocks, weights, kdiag, fluid_a, fluid_b, metal, coef):
    local = jnp.einsum('fgabc,gabc->fabc', blocks, field, precision=lax.Precision.HIGHEST)
    padded = jnp.pad(field, ((0, 0), (1, 1), (1, 1), (0, 0)))
    beside = weights[0][None] * padded[:, :-2, 1:-1] + weights[1][None] * padded[:, 2:, 1:-1]
    beside = beside + weights[2][None] * padded[:, 1:-1, :-2] + weights[3][None] * padded[:, 1:-1, 2:]
    beside = beside + weights[4][None] * jnp.roll(field, 1, axis=3) + weights[5][None] * jnp.roll(field, -1, axis=3)
    inflow = jnp.zeros((NA, NB, NC), jnp.float32).at[fluid_a, fluid_b].add(coef * metal_u[metal])
    image_f = (local - beside).at[5].add(-inflow)
    upad = jnp.pad(metal_u, ((1, 1), (0, 0)))
    sink = jnp.zeros((NSOL, NC), jnp.float32).at[metal].add(coef * field[5, fluid_a, fluid_b])
    image_s = (4.0 + kdiag) * metal_u - (upad[:-2] + upad[2:] + jnp.roll(metal_u, 1, axis=1) + jnp.roll(metal_u, -1, axis=1)) - sink
    return (image_f, image_s)

def inner(left, right):
    return jnp.sum(left[0] * right[0]) + jnp.sum(left[1] * right[1])

def least_squares(hess, beta, steps):
    cos_list, sin_list, upper = ([], [], [])
    rhs_g = [beta] + [jnp.float32(0.0) for _ in range(steps)]
    for j in range(steps):
        column = [hess[i][j] for i in range(j + 2)]
        for i in range(j):
            top = cos_list[i] * column[i] + sin_list[i] * column[i + 1]
            column[i + 1] = -sin_list[i] * column[i] + cos_list[i] * column[i + 1]
            column[i] = top
        radius = jnp.sqrt(column[j] * column[j] + column[j + 1] * column[j + 1])
        cos_now = column[j] / radius
        sin_now = column[j + 1] / radius
        column[j] = radius
        rhs_g[j + 1] = -sin_now * rhs_g[j]
        rhs_g[j] = cos_now * rhs_g[j]
        cos_list.append(cos_now)
        sin_list.append(sin_now)
        upper.append(column[:j + 1])
    coeffs = [None] * steps
    for j in range(steps - 1, -1, -1):
        total = rhs_g[j]
        for k in range(j + 1, steps):
            total = total - upper[k][j] * coeffs[k]
        coeffs[j] = total / upper[j][j]
    return coeffs

def reference(rhs_fluid, rhs_solid, blocks, weights, kdiag, wall_fluid, wall_solid, wall_coef):
    fluid_a, fluid_b, metal = patch_index(wall_fluid, wall_solid)
    coef = wall_coef.reshape(-1, NC)
    start = (rhs_fluid, rhs_solid)
    beta = jnp.sqrt(inner(start, start))
    basis = [(rhs_fluid / beta, rhs_solid / beta)]
    hess = [[jnp.float32(0.0) for _ in range(KRYLOV)] for _ in range(KRYLOV + 1)]
    for j in range(KRYLOV):
        image_f, image_s = apply_all(basis[j][0], basis[j][1], blocks, weights, kdiag, fluid_a, fluid_b, metal, coef)
        image = (image_f, image_s)
        values = [inner(basis[i], image) for i in range(j + 1)]
        for i in range(j + 1):
            hess[i][j] = values[i]
            image_f = image_f - values[i] * basis[i][0]
            image_s = image_s - values[i] * basis[i][1]
        rest = jnp.sqrt(inner((image_f, image_s), (image_f, image_s)))
        hess[j + 1][j] = rest
        basis.append((image_f / rest, image_s / rest))
    coeffs = least_squares(hess, beta, KRYLOV)
    x_fluid = jnp.zeros_like(rhs_fluid)
    x_solid = jnp.zeros_like(rhs_solid)
    for j in range(KRYLOV):
        x_fluid = x_fluid + coeffs[j] * basis[j][0]
        x_solid = x_solid + coeffs[j] * basis[j][1]
    return (x_fluid, x_solid)
```

```python
import functools
import math

import jax
import jax.numpy as jnp
from jax import lax
from jax.experimental import pallas as pl
from jax.experimental.pallas import tpu as pltpu
from jax.sharding import PartitionSpec as P

KRYLOV = 6
AXES = ("span", "flow")
F32 = jnp.float32
HI = lax.Precision.HIGHEST
PAIRS = [(i, j) for i in range(KRYLOV + 1) for j in range(i, KRYLOV + 1)]


def call(kernel, outs, *args, smem=()):
    outs = [jax.ShapeDtypeStruct(shape, F32) for shape in outs]
    moved = sum(math.prod(a.shape) for a in args) + sum(math.prod(o.shape) for o in outs)
    return pl.pallas_call(
        kernel,
        out_shape=outs,
        in_specs=[
            pl.BlockSpec(memory_space=pltpu.SMEM if n in smem else pltpu.VMEM)
            for n in range(len(args))
        ],
        out_specs=[pl.BlockSpec(memory_space=pltpu.VMEM)] * len(outs),
        cost_estimate=pl.CostEstimate(flops=8 * moved, bytes_accessed=4 * moved, transcendentals=0),
    )(*args)


def place():
    i, q = lax.axis_index("span"), lax.axis_index("flow")
    last_i, last_q = lax.axis_size("span") - 1, lax.axis_size("flow") - 1
    return (i % 2 == 1, i == 0, i == last_i), (q % 2 == 1, q == 0, q == last_q)


def iota(shape, dim):
    return lax.broadcasted_iota(jnp.int32, shape, dim)


def rows_sum(x):
    return jnp.sum(x, axis=0, keepdims=True)


def load(ref):
    return [[ref[f, a] for a in range(ref.shape[1])] for f in range(ref.shape[0])]


def store(ref, tiles):
    for f, line in enumerate(tiles):
        for a, tile in enumerate(line):
            ref[f, a] = tile


def send(tiles, flow_a, flow_b, span_a, span_b):
    (odd_i, _, _), (odd_q, _, _) = place()
    rows_a, rows_b = len(tiles[0]), tiles[0][0].shape[0]
    for f, line in enumerate(tiles):
        for a, tile in enumerate(line):
            first, last = tile[0:1], tile[rows_b - 1 : rows_b]
            row = f * rows_a + a
            flow_a[row : row + 1] = jnp.where(odd_q, first, last)
            flow_b[row : row + 1] = jnp.where(odd_q, last, first)
        span_a[f] = jnp.where(odd_i, line[0], line[-1])
        span_b[f] = jnp.where(odd_i, line[-1], line[0])


def sides(got_a, got_b, where):
    odd, first, last = where
    zero = jnp.zeros_like(got_a)
    before = jnp.where(first, zero, jnp.where(odd, got_a, got_b))
    after = jnp.where(last, zero, jnp.where(odd, got_b, got_a))
    return before, after


def receive(flow_a, flow_b, span_a, span_b, fields):
    where_i, where_q = place()
    left, right = sides(flow_a[...], flow_b[...], where_q)
    low, high = zip(*[sides(span_a[f], span_b[f], where_i) for f in range(fields)])
    return left, right, low, high


def fluid(tiles, halo, blocks, weights, inflow):
    left, right, low, high = halo
    fields, rows_a = len(tiles), len(tiles[0])
    rows_b, width = tiles[0][0].shape
    at_first = iota((rows_b, width), 0) == 0
    at_last = iota((rows_b, width), 0) == rows_b - 1
    image = [[None] * rows_a for _ in range(fields)]
    for a in range(rows_a):
        face = [weights[d, a] for d in range(6)]
        for f in range(fields):
            tile = tiles[f][a]
            row = f * rows_a + a
            local = blocks[f, 0, a] * tiles[0][a]
            for g in range(1, fields):
                local = local + blocks[f, g, a] * tiles[g][a]
            below = tiles[f][a - 1] if a else low[f]
            above = tiles[f][a + 1] if a < rows_a - 1 else high[f]
            up = jnp.where(at_first, left[row : row + 1], pltpu.roll(tile, 1, 0))
            down = jnp.where(at_last, right[row : row + 1], pltpu.roll(tile, rows_b - 1, 0))
            beside = face[0] * below + face[1] * above
            beside = beside + face[2] * up + face[3] * down
            beside = beside + face[4] * pltpu.roll(tile, 1, 1)
            beside = beside + face[5] * pltpu.roll(tile, width - 1, 1)
            out = local - beside
            if f == fields - 1:
                out = out - inflow[a]
            image[f][a] = out
    return image


def wall_row(tiles, wall):
    total = None
    for a in range(len(tiles[-1])):
        part = rows_sum(wall[a] * tiles[-1][a])
        total = part if total is None else total + part
    return total


def inflow_of(wall, row):
    return [wall[a] * row for a in range(wall.shape[0])]


def metal(u, kdiag, before=None, after=None):
    rows, width = u.shape
    at = iota(u.shape, 0)
    up = jnp.where(at == 0, 0.0 if before is None else before, pltpu.roll(u, 1, 0))
    down = jnp.where(at == rows - 1, 0.0 if after is None else after, pltpu.roll(u, rows - 1, 0))
    return (4.0 + kdiag) * u - (up + down + pltpu.roll(u, 1, 1) + pltpu.roll(u, width - 1, 1))


def shifted(image, tiles, theta, inverse):
    return [
        [(y - theta * x) * inverse for y, x in zip(ys, xs)] for ys, xs in zip(image, tiles)
    ]


def dot_rows(left, right):
    total = None
    for xs, ys in zip(left, right):
        for x, y in zip(xs, ys):
            total = x * y if total is None else total + x * y
    return rows_sum(total)


def lanes(rows, width):
    pad = -len(rows) % 8
    stack = jnp.concatenate(rows + [jnp.zeros_like(rows[0])] * pad, axis=0)
    sums = jnp.sum(stack, axis=1, keepdims=True)
    shape = (stack.shape[0], width)
    return rows_sum(jnp.where(iota(shape, 0) == iota(shape, 1), sums, 0.0))


def start_kernel(scale, patch, pair, rhs, solid, coef, w0, wall, mine, fa, fb, sa, sb):
    fields, rows_a, rows_b, width = rhs.shape
    tiles = [[t * scale for t in line] for line in load(rhs)]
    store(w0, tiles)
    send(tiles, fa, fb, sa, sb)
    (odd_i, _, _), _ = place()
    rows = solid.shape[0]
    first = jnp.broadcast_to(solid[0:1] * scale, (rows_b, width))
    last = jnp.broadcast_to(solid[rows - 1 : rows] * scale, (rows_b, width))
    sa[fields] = jnp.where(odd_i, first, last)
    sb[fields] = jnp.where(odd_i, last, first)
    for a in range(rows_a):
        hit = iota((rows_b, width), 0) + a * rows_b == patch[0, 0]
        wall[a] = jnp.where(hit, coef[...], 0.0)
    mine[...] = (iota((rows, width), 0) == pair[0, 0]).astype(F32)


def first_kernel(
    scale, w0, fa, fb, sa, sb, blocks, weights, wall, mine, solid, kdiag,
    w1, fa1, fb1, sa1, sb1, own1, packed,
):
    fields = w0.shape[0]
    where_i, _ = place()
    tiles = load(w0)
    u = solid[...] * scale
    mask = mine[...]
    own0 = rows_sum(mask * u)
    image = fluid(
        tiles, receive(fa, fb, sa, sb, fields), blocks, weights, inflow_of(wall, own0)
    )
    store(w1, image)
    send(image, fa1, fb1, sa1, sb1)
    before, after = sides(sa[fields][0:1], sb[fields][0:1], where_i)
    p0 = wall_row(tiles, wall)
    own = rows_sum(mask * metal(u, kdiag[...], before, after)) - p0
    own1[...] = own
    p1 = wall_row(image, wall)
    kd = rows_sum(mask * kdiag[...])
    rows, width = u.shape
    which = rows_sum(mask * iota(u.shape, 0).astype(F32)) + (
        lax.axis_index("span") * rows
    ).astype(F32)
    stats = lanes(
        [
            dot_rows(tiles, tiles) + own0 * own0,
            dot_rows(tiles, image) + own0 * own,
            dot_rows(image, image) + own * own,
        ],
        width,
    )
    block = jnp.concatenate(
        [p0, p1, own0, kd, which, stats, jnp.zeros((2, width), F32)], axis=0
    )
    packed[...] = jnp.broadcast_to(block[None], packed.shape)


def raw_kernel(w, fa, fb, sa, sb, blocks, weights, wall, own, out, fa1, fb1, sa1, sb1):
    tiles = load(w)
    halo = receive(fa, fb, sa, sb, w.shape[0])
    image = fluid(tiles, halo, blocks, weights, inflow_of(wall, own[...]))
    store(out, image)
    send(image, fa1, fb1, sa1, sb1)


def own_row(full, mask):
    rows = mask.shape[0]
    at = pl.multiple_of(lax.axis_index("span") * rows, rows)
    return rows_sum(mask[...] * full[pl.ds(at, rows)])


def turn(pick, slots):
    return lax.dot_general(
        pick, slots, (((0,), (0,)), ((), ())), precision=HI, preferred_element_type=F32
    )


def metal_kernel(got, mine, scal, pick, u0, u1, u2, kd, work, own2, next2):
    slots, _, width = got.shape
    at = jnp.broadcast_to(got[:, 4, :][:, 0:1], (slots, slots)).astype(jnp.int32)
    pick[...] = (at == iota((slots, slots), 1)).astype(F32)
    order = pick[...]
    stats = rows_sum(got[:, 5, :])
    norm = stats[:, 0:1]
    theta = stats[:, 1:2] / norm
    square = stats[:, 2:3] / norm - theta * theta
    sigma = jnp.where(square > 0.0, jnp.sqrt(jnp.maximum(square, 0.0)), 1.0)
    theta = jnp.broadcast_to(theta, (1, width))
    sigma = jnp.broadcast_to(sigma, (1, width))
    inverse = 1.0 / sigma
    scal[...] = jnp.concatenate([theta, inverse, sigma, jnp.zeros((5, width), F32)], axis=0)
    wall0, wall1 = turn(order, got[:, 0, :]), turn(order, got[:, 1, :])
    start, diag = turn(order, got[:, 2, :]), turn(order, got[:, 3, :])
    one = metal(start, diag) - wall0
    two = metal(one, diag) - wall1
    basis1 = (one - theta * start) * inverse
    basis2 = ((two - theta * one) * inverse - theta * basis1) * inverse
    u0[...] = start
    u1[...] = basis1
    u2[...] = basis2
    kd[...] = diag
    own2[...] = own_row(u2, mine)
    work[...] = (metal(basis2, diag) - theta * basis2) * inverse
    next2[...] = own_row(work, mine)


def third_kernel(
    w0, w1, w2, fa0, fb0, sa0, sb0, fa1, fb1, sa1, sb1, fa2, fb2, sa2, sb2,
    blocks, weights, wall, scal, own2, next2,
    b1, b2, w3, fa3, fb3, sa3, sb3, own3, packed,
):
    fields = w0.shape[0]
    theta, inverse = scal[0:1], scal[1:2]

    def recombine(x0, x1, x2):
        y1 = (x1 - theta * x0) * inverse
        return y1, ((x2 - theta * x1) * inverse - theta * y1) * inverse

    tiles1, tiles2 = [], []
    for l0, l1, l2 in zip(load(w0), load(w1), load(w2)):
        pairs = [recombine(*x) for x in zip(l0, l1, l2)]
        tiles1.append([p[0] for p in pairs])
        tiles2.append([p[1] for p in pairs])
    store(b1, tiles1)
    store(b2, tiles2)
    where_i, where_q = place()
    mix = lambda *x: recombine(*x)[1]
    left, right = sides(
        mix(fa0[...], fa1[...], fa2[...]), mix(fb0[...], fb1[...], fb2[...]), where_q
    )
    low, high = zip(*[
        sides(mix(sa0[f], sa1[f], sa2[f]), mix(sb0[f], sb1[f], sb2[f]), where_i)
        for f in range(fields)
    ])
    image = fluid(
        tiles2, (left, right, low, high), blocks, weights, inflow_of(wall, own2[...])
    )
    tiles3 = shifted(image, tiles2, theta, inverse)
    store(w3, tiles3)
    send(tiles3, fa3, fb3, sa3, sb3)
    p2, p3 = wall_row(tiles2, wall), wall_row(tiles3, wall)
    own3[...] = next2[...] - p2 * inverse
    block = jnp.concatenate([p2, p3], axis=0)
    packed[...] = jnp.broadcast_to(block[None], packed.shape)


def step_kernel(
    w, fa, fb, sa, sb, blocks, weights, wall, scal, own, out, fa1, fb1, sa1, sb1
):
    theta, inverse = scal[0:1], scal[1:2]
    tiles = load(w)
    halo = receive(fa, fb, sa, sb, w.shape[0])
    image = fluid(tiles, halo, blocks, weights, inflow_of(wall, own[...]))
    tiles = shifted(image, tiles, theta, inverse)
    store(out, tiles)
    send(tiles, fa1, fb1, sa1, sb1)


def metal_step(u, diag, wall, theta, inverse):
    return (metal(u, diag) - wall - theta * u) * inverse


def second_metal_kernel(got, pick, kd, u2, scal, mine, u3, u4, work, own4, next4):
    theta, inverse = scal[0:1], scal[1:2]
    order, diag = pick[...], kd[...]
    three = metal_step(u2[...], diag, turn(order, got[:, 0, :]), theta, inverse)
    four = metal_step(three, diag, turn(order, got[:, 1, :]), theta, inverse)
    u3[...] = three
    u4[...] = four
    own4[...] = own_row(u4, mine)
    work[...] = (metal(four, diag) - theta * four) * inverse
    next4[...] = own_row(work, mine)


def fifth_kernel(
    w, fa, fb, sa, sb, blocks, weights, wall, scal, own, following,
    out, fa1, fb1, sa1, sb1, own5,
):
    step_kernel(
        w, fa, fb, sa, sb, blocks, weights, wall, scal, own, out, fa1, fb1, sa1, sb1
    )
    own5[...] = following[...] - wall_row(load(w), wall) * scal[1:2]


def last_kernel(
    w0, w1, w2, w3, w4, w5, fa, fb, sa, sb, blocks, weights, wall, scal, own, packed
):
    theta, inverse = scal[0:1], scal[1:2]
    width = w0.shape[3]
    basis = [load(w) for w in (w0, w1, w2, w3, w4, w5)]
    halo = receive(fa, fb, sa, sb, w0.shape[0])
    image = fluid(basis[5], halo, blocks, weights, inflow_of(wall, own[...]))
    basis.append(shifted(image, basis[5], theta, inverse))
    sums = lanes([dot_rows(basis[i], basis[j]) for i, j in PAIRS], width)
    block = jnp.concatenate(
        [sums, wall_row(basis[4], wall), wall_row(basis[5], wall), jnp.zeros_like(sums)], axis=0
    )
    packed[...] = jnp.broadcast_to(block[None], packed.shape)


def solve(gram, theta, sigma):
    n = KRYLOV
    g = lambda i, j: gram[min(i, j), max(i, j)]
    mat = [[None] * n for _ in range(n)]
    vec = []
    for j in range(n):
        for k in range(j + 1):
            mat[j][k] = (
                sigma * (sigma * g(j + 1, k + 1) + theta * (g(j + 1, k) + g(j, k + 1)))
                + theta * theta * g(j, k)
            )
        vec.append(sigma * g(j + 1, 0) + theta * g(j, 0))
    inv = []
    for j in range(n):
        inv.append(1.0 / mat[j][j])
        for i in range(j + 1, n):
            factor = mat[i][j] * inv[j]
            for k in range(j + 1, i + 1):
                mat[i][k] = mat[i][k] - factor * mat[k][j]
            vec[i] = vec[i] - factor * vec[j]
    out = [None] * n
    for j in range(n - 1, -1, -1):
        total = vec[j]
        for k in range(j + 1, n):
            total = total - mat[k][j] * out[k]
        out[j] = total * inv[j]
    return out


def end_kernel(
    scale, got, pick, kd, scal, u0, u1, u2, u3, u4, w0, w1, w2, w3, w4, w5,
    x_fluid, x_solid, work,
):
    theta, inverse = scal[0:1], scal[1:2]
    width = w0.shape[3]
    order, diag = pick[...], kd[...]
    u = [r[...] for r in (u0, u1, u2, u3, u4)]
    u.append(metal_step(u[4], diag, turn(order, got[:, 1, :]), theta, inverse))
    u.append(metal_step(u[5], diag, turn(order, got[:, 2, :]), theta, inverse))
    sums = rows_sum(got[:, 0, :]) + lanes([rows_sum(u[i] * u[j]) for i, j in PAIRS], width)
    gram = {pair: sums[:, n : n + 1] for n, pair in enumerate(PAIRS)}
    coeffs = solve(gram, scal[0:1, 0:1], scal[2:3, 0:1])
    coeffs = [jnp.broadcast_to(c * (1.0 / scale), (1, width)) for c in coeffs]
    basis = (w0, w1, w2, w3, w4, w5)
    for f in range(w0.shape[0]):
        for a in range(w0.shape[1]):
            total = coeffs[0] * w0[f, a]
            for j in range(1, KRYLOV):
                total = total + coeffs[j] * basis[j][f, a]
            x_fluid[f, a] = total
    total = coeffs[0] * u[0]
    for j in range(1, KRYLOV):
        total = total + coeffs[j] * u[j]
    work[...] = total
    rows = x_solid.shape[0]
    at = pl.multiple_of(lax.axis_index("span") * rows, rows)
    x_solid[...] = work[pl.ds(at, rows)]


def pairings(n_span, n_flow):
    even = lambda n: [(i, i ^ 1) for i in range(n)]
    odd = lambda n: [(i, (i + 1) % n if i % 2 else (i - 1) % n) for i in range(n)]
    both = []
    for i in range(n_span):
        for q in range(n_flow):
            other = i + 1 if i % 2 else i - 1
            to = (other, q) if 0 <= other < n_span else (i, q ^ 1)
            both.append((i * n_flow + q, to[0] * n_flow + to[1]))
    return even(n_flow), odd(n_flow), even(n_span), both


def shards(rhs_fluid, rhs_solid, blocks, weights, kdiag, wall_fluid, wall_solid, wall_coef):
    n_span, n_flow = lax.axis_size("span"), lax.axis_size("flow")
    fields, rows_a, rows_b, width = rhs_fluid.shape
    rows = rhs_solid.shape[0]
    devices = n_span * n_flow
    count = fields * rows_a * rows_b * width * devices + rows * width * n_span
    scale = 2.0 ** -math.ceil(math.log2(6.0 * math.sqrt(count)))
    flow_a, flow_b, span_a, span_b = pairings(n_span, n_flow)

    def exchange(fa, fb, sa, sb):
        return (
            lax.ppermute(fa, "flow", flow_a),
            lax.ppermute(fb, "flow", flow_b),
            lax.ppermute(sa, "span", span_a),
            lax.ppermute(sb, AXES, span_b),
        )

    def gather(packed):
        return lax.all_to_all(packed, AXES, 0, 0)

    tile = rhs_fluid.shape
    row = (1, width)
    full = (devices, width)
    edges = [(fields * rows_a, width)] * 2 + [(fields, rows_b, width)] * 2
    edges0 = edges[:2] + [(fields + 1, rows_b, width)] * 2

    w0, wall, mine, *out = call(
        functools.partial(start_kernel, scale),
        [tile, (rows_a, rows_b, width), (rows, width)] + edges0,
        wall_fluid, wall_solid, rhs_fluid, rhs_solid, wall_coef[0],
        smem=(0, 1),
    )
    halo0 = exchange(*out)
    w1, *out, own1, packed = call(
        functools.partial(first_kernel, scale),
        [tile] + edges + [row, (devices, 8, width)],
        w0, *halo0, blocks, weights, wall, mine, rhs_solid, kdiag,
    )
    halo1 = exchange(*out)
    got = gather(packed)
    w2, *out = call(raw_kernel, [tile] + edges, w1, *halo1, blocks, weights, wall, own1)
    halo2 = exchange(*out)
    scal, pick, u0, u1, u2, kd, _, own2, next2 = call(
        metal_kernel,
        [(8, width), (devices, devices)] + [full] * 5 + [row, row],
        got, mine,
    )
    b1, b2, w3, *out, own3, packed = call(
        third_kernel,
        [tile] * 3 + edges + [row, (devices, 2, width)],
        w0, w1, w2, *halo0, *halo1, *halo2, blocks, weights, wall, scal, own2, next2,
    )
    halo3 = exchange(*out)
    got = gather(packed)
    w4, *out = call(
        step_kernel, [tile] + edges, w3, *halo3, blocks, weights, wall, scal, own3
    )
    halo4 = exchange(*out)
    u3, u4, _, own4, next4 = call(
        second_metal_kernel, [full] * 3 + [row, row], got, pick, kd, u2, scal, mine
    )
    w5, *out, own5 = call(
        fifth_kernel,
        [tile] + edges + [row],
        w4, *halo4, blocks, weights, wall, scal, own4, next4,
    )
    halo5 = exchange(*out)
    (packed,) = call(
        last_kernel,
        [(devices, 4, width)],
        w0, b1, b2, w3, w4, w5, *halo5, blocks, weights, wall, scal, own5,
    )
    got = gather(packed)
    x_fluid, x_solid, _ = call(
        functools.partial(end_kernel, scale),
        [tile, (rows, width), full],
        got, pick, kd, scal, u0, u1, u2, u3, u4, w0, b1, b2, w3, w4, w5,
    )
    return x_fluid, x_solid


def solution(mesh):
    in_specs = (
        P(None, "span", "flow", None),
        P("span", None),
        P(None, None, "span", "flow", None),
        P(None, "span", "flow", None),
        P("span", None),
        P("span", "flow"),
        P("span", "flow"),
        P("span", "flow", None),
    )
    out_specs = (P(None, "span", "flow", None), P("span", None))
    return jax.shard_map(shards, mesh=mesh, in_specs=in_specs, out_specs=out_specs, check_vma=False)
```
